32 devices in a mesh: gx: 8 (over z, y), gz: 4 (over x, core).
Axes of the slice: x: 2, y: 2, z: 4, core: 2. Of those that a mesh axis runs over, the one named last changes fastest.
Arguments:
- volume: float32 [256, 64, 1024], P('gz', None, 'gx'), may hold values from -96 to 96
- centers: float32 [8], replicated, may hold values from -1.5 to 1.5
- sharpness: float32 [8], replicated, may hold values from 0.5 to 4
- extinction: float32 [8], replicated, may hold values from 0.2 to 3
- colors: float32 [3, 8], replicated, may hold values from 0 to 1
Outputs:
- image_tiles: float32 [4, 64, 1024], P(None, 'gz', 'gx')
The draws below stay inside these ranges and needn't reach their ends.
All inputs are finite; a program needn't handle non-finite values.
Results may differ from the reference program's by a relative error of at most 0.00002.
Values sent between devices are 32-bit elements; how exact they have to be, the bound alone decides.
A program may use at most 64 MiB of HBM per device.

```python
import math
import jax
import jax.numpy as jnp
from jax import lax

BY = 64
K = 8
NX = 1024
NZ = 256


def block_scale(stream_key, shape, cuts, smallest, top_value):
    loudness, own = 1.0, jax.random.fold_in(stream_key, 6)
    for position, parts in cuts:
        steps = jnp.exp(jax.random.uniform(jax.random.fold_in(own, position), (parts,), jnp.float32, smallest / len(cuts), top_value / len(cuts)))
        loudness = loudness * jnp.repeat(steps, shape[position] // parts).reshape([-1 if axis == position else 1 for axis in range(len(shape))])
    return loudness


def bell_draw(own_key, dims, deviation, most, split=(), held_as=jnp.bfloat16):
    array = jax.random.normal(own_key, dims, jnp.float32) * deviation
    if len(split) > 0:
        array = block_scale(own_key, dims, split, -0.22, 0.18) * array
    return jnp.clip(array, min=-most, max=most).astype(held_as)


def setup_inputs(seed: int = 0) -> dict:
    keys = jax.random.split(jax.random.key(seed), 6)
    volume = bell_draw(keys[0], (NZ, BY, NX), 16.0, 96.0, ((0, 4), (2, 8)), jnp.float32)
    centers = jnp.clip(jax.random.uniform(keys[1], (K,), jnp.float32, -1.5, 1.5), -1.5, 1.5)
    sharpness = jnp.clip(jnp.exp(jax.random.uniform(keys[2], (K,), jnp.float32, math.log(0.5), math.log(4.0))), 0.5, 4.0)
    extinction = jnp.clip(jnp.exp(jax.random.uniform(keys[3], (K,), jnp.float32, math.log(0.2), math.log(3.0))), 0.2, 3.0)
    colors = jnp.clip(jax.random.uniform(keys[4], (3, K), jnp.float32, 0.0, 1.0), 0.0, 1.0)
    return {"volume": volume, "centers": centers, "sharpness": sharpness, "extinction": extinction, "colors": colors}


def tap_weights():
    raw = [math.exp(-(j * j) / 8.0) for j in range(-4, 5)]
    whole = sum(raw)
    return [value / whole for value in raw]


def valid_pass(field, axis, count):
    weights = tap_weights()
    total = weights[0] * lax.slice_in_dim(field, 0, count, axis=axis)
    for offset in range(1, 9):
        total = total + weights[offset] * lax.slice_in_dim(field, offset, offset + count, axis=axis)
    return total


def padded_pass(field, axis):
    widths = [(0, 0), (0, 0), (0, 0)]
    widths[axis] = (4, 4)
    return valid_pass(jnp.pad(field, widths), axis, field.shape[axis])


def transfer(density, centers, sharpness, extinction, colors):
    sigma = jnp.zeros_like(density)
    emits = [jnp.zeros_like(density), jnp.zeros_like(density), jnp.zeros_like(density)]
    for comp in range(centers.shape[0]):
        offset = density - centers[comp]
        bump = jnp.exp(-sharpness[comp] * offset * offset)
        sigma = sigma + extinction[comp] * bump
        for chan in range(3):
            emits[chan] = emits[chan] + colors[chan, comp] * bump
    return sigma, emits


def reference(volume, centers, sharpness, extinction, colors):
    smoothed = padded_pass(volume, 0)
    smoothed = padded_pass(smoothed, 2)
    density = padded_pass(smoothed, 1)
    sigma, emits = transfer(density, centers, sharpness, extinction, colors)
    tau = sigma / jnp.float32(volume.shape[0])
    cumul = jnp.cumsum(tau, axis=0)
    before = cumul - tau
    weight = jnp.exp(-before) * (-jnp.expm1(-tau))
    planes = [jnp.sum(weight * emits[chan], axis=0) for chan in range(3)]
    planes.append(jnp.exp(-cumul[-1]))
    return jnp.stack(planes, axis=0)
```

```python
import functools
import math

import jax
import jax.numpy as jnp
import numpy as np
from jax import lax
from jax.experimental import pallas as pl
from jax.experimental.pallas import tpu as pltpu
from jax.sharding import PartitionSpec as P

F32 = jnp.float32
BF16 = jnp.bfloat16
MESH = pl.DeviceIdType.MESH
HALO = 4
PIECE = 2 * HALO


def tap_weights():
    raw = [math.exp(-(j * j) / 8.0) for j in range(-4, 5)]
    whole = sum(raw)
    return [value / whole for value in raw]


def split_const(matrix):
    high = matrix.astype(np.float32).astype(BF16)
    low = (matrix - high.astype(np.float64)).astype(np.float32).astype(BF16)
    return high, low


def band(count, shift, rows):
    weights = tap_weights()
    matrix = np.zeros((rows, count), np.float64)
    for source in range(rows):
        for target in range(count):
            offset = shift(source) - target
            if -4 <= offset <= 4:
                matrix[source, target] = weights[offset + 4]
    return matrix


def constants(rows, columns):
    high, low = split_const(band(rows, lambda i: i, rows).T)
    left = np.concatenate([high, high, low], axis=1)
    high, low = split_const(band(columns, lambda i: i, columns))
    main = np.concatenate([high, high, low], axis=0)
    side = np.zeros((columns, columns), np.float64)
    side[:PIECE] = band(columns, lambda i: i - HALO if i < HALO else columns + i - HALO, PIECE)
    high, low = split_const(side)
    edge = np.concatenate([high, high, low], axis=0)
    return left, main, edge


def split(value):
    high = value.astype(BF16)
    low = (value - high.astype(F32)).astype(BF16)
    return high, low


def rows_pass(left, slab):
    high, low = split(slab)
    return jnp.dot(left, jnp.concatenate([high, low, high], axis=0), preferred_element_type=F32)


def columns_pass(rows, matrix):
    high, low = split(rows)
    return jnp.dot(jnp.concatenate([high, low, high], axis=1), matrix, preferred_element_type=F32)


def kernel(nx, nz, terms, volume, centers, sharpness, extinction, colors, left_ref, main_ref, edge_ref,
           out_ref, vol, packed, from_left, from_right, layers, smooth, sent, pieces,
           load_sem, left_send, left_recv, right_send, right_recv, layer_send, layer_recv, image_send, image_recv):
    depth, rows, columns = vol.shape
    per_group = columns // PIECE
    groups = depth // per_group
    row_block = rows // nz
    ix = lax.axis_index("gx")
    iz = lax.axis_index("gz")
    has_left, has_right = ix > 0, ix < nx - 1
    has_front, has_back = iz > 0, iz < nz - 1

    barrier = pltpu.get_barrier_semaphore()

    def greet(x, z):
        pl.semaphore_signal(barrier, inc=1, device_id={"gx": x, "gz": z}, device_id_type=MESH)

    loads = []
    for g in range(groups):
        span = pl.ds(g * per_group, per_group)
        loads.append(pltpu.make_async_copy(volume.at[span], vol.at[span], load_sem.at[g]))
        loads[-1].start()

    for step in range(1, nz):
        greet(ix, lax.rem(iz + step, nz))
    for here, x in ((has_left, ix - 1), (has_right, ix + 1)):
        pl.when(here)(functools.partial(greet, x, iz))
        pl.when(here & has_front)(functools.partial(greet, x, iz - 1))
        pl.when(here & has_back)(functools.partial(greet, x, iz + 1))
    sides = has_left.astype(jnp.int32) + has_right.astype(jnp.int32)
    ends = has_front.astype(jnp.int32) + has_back.astype(jnp.int32)

    lane = lax.broadcasted_iota(jnp.int32, (rows, columns), 1)

    def pack(g):
        def body(m, total):
            turned = pltpu.roll(vol[g * per_group + m], lax.rem(PIECE * m + HALO, columns), axis=1)
            return jnp.where(lane // PIECE == m, turned, total)

        total = jnp.zeros((rows, columns), F32)
        for m in range(per_group):
            total = body(m, total)
        packed[g] = total

    def remote(source, target, send, recv, x, z):
        return pltpu.make_async_remote_copy(
            src_ref=source, dst_ref=target, send_sem=send, recv_sem=recv,
            device_id={"gx": x, "gz": z}, device_id_type=MESH,
        )

    last = groups - 1
    copies = []

    def launch(condition, copy):
        copies.append((condition, copy))
        pl.when(condition)(copy.start)

    for g in range(groups):
        loads[g].wait()
        pack(g)
        if g == 0:
            pl.semaphore_wait(barrier, nz - 1 + sides * (1 + ends))
        for here, x, inbox, send, recv in (
            (has_right, ix + 1, from_left, left_send, left_recv),
            (has_left, ix - 1, from_right, right_send, right_recv),
        ):
            launch(here, remote(packed.at[g], inbox.at[g + 1], send.at[g + 1], recv.at[g + 1], x, iz))
            if g == 0:
                slot = groups + 1
                launch(here & has_front, remote(packed.at[0], inbox.at[slot], send.at[slot], recv.at[slot], x, iz - 1))
            if g == last:
                launch(here & has_back, remote(packed.at[last], inbox.at[0], send.at[0], recv.at[0], x, iz + 1))
        if g == 0:
            launch(has_back, remote(volume.at[pl.ds(depth - HALO, HALO)], layers.at[0], layer_send.at[0], layer_recv.at[0], ix, iz + 1))
            launch(has_front, remote(volume.at[pl.ds(0, HALO)], layers.at[1], layer_send.at[1], layer_recv.at[1], ix, iz - 1))

    left = left_ref[...]

    def plane_pass(source, start, target):
        wide = jnp.concatenate([source[start + i] for i in range(HALO)], axis=1)
        wide = rows_pass(left, wide)
        tall = jnp.concatenate([wide[:, i * columns:(i + 1) * columns] for i in range(HALO)], axis=0)
        tall = columns_pass(tall, main_ref[...])
        for i in range(HALO):
            smooth[target + i] = tall[i * rows:(i + 1) * rows]

    @pl.loop(0, depth // HALO)
    def _(step):
        plane_pass(vol, step * HALO, step * HALO + HALO)

    def arrive(condition, copy, inbox):
        pl.when(condition)(copy.wait_recv)

        @pl.when(jnp.logical_not(condition))
        def _():
            inbox[...] = jnp.zeros(inbox.shape, F32)

    for end, here in ((0, has_front), (1, has_back)):
        arrive(here, remote(layers.at[end], layers.at[end], layer_send.at[end], layer_recv.at[end], ix, iz), layers.at[end])
        plane_pass(layers.at[end], 0, end * (depth + HALO))

    for g in range(groups + 2):
        beside = has_front if g == 0 else has_back if g == groups + 1 else None
        for here, inbox, send, recv in (
            (has_left, from_left, left_send, left_recv),
            (has_right, from_right, right_send, right_recv),
        ):
            both = here if beside is None else here & beside
            arrive(both, remote(inbox.at[g], inbox.at[g], send.at[g], recv.at[g], ix, iz), inbox.at[g])

    def edges(g, first, count, target):
        piece = jnp.where(lane % PIECE < HALO, from_left[g], from_right[g])
        piece = rows_pass(left, piece)
        for m in range(first, first + count, HALO):
            tall = jnp.concatenate(
                [pltpu.roll(piece, (columns - PIECE * (m + i)) % columns, axis=1) for i in range(HALO)], axis=0
            )
            tall = columns_pass(tall, edge_ref[...])
            for i in range(HALO):
                at = target + m - first + i
                smooth[at] = smooth[at] + tall[i * rows:(i + 1) * rows]

    edges(0, per_group - HALO, HALO, 0)
    edges(groups + 1, 0, HALO, depth + HALO)

    @pl.loop(0, groups)
    def _(g):
        edges(g + 1, 0, per_group, g * per_group + HALO)

    taps = tap_weights()
    comps = centers.shape[0]
    log2e = math.log2(math.e)
    cells = depth * nz
    middle = [centers[k] for k in range(comps)]
    fall = [sharpness[k] * F32(-log2e) for k in range(comps)]
    absorb = [extinction[k] * F32(1.0 / cells) for k in range(comps)]
    shine = [[colors[c, k] for k in range(comps)] for c in range(3)]
    unroll = 2

    def render(row):
        start = pl.multiple_of(row * row_block, row_block)

        def body(step, carry):
            trans, red, green, blue = carry
            z = step * unroll

            def load(j):
                return smooth[pl.ds(z + j, unroll), pl.ds(start, row_block), :]

            density = taps[4] * load(4)
            for j in range(4):
                density = density + taps[j] * (load(j) + load(8 - j))
            tau = None
            for k in range(comps):
                offset = density - middle[k]
                bump = jnp.exp2(fall[k] * offset * offset)
                if tau is None:
                    tau = absorb[k] * bump
                    emits = [shine[c][k] * bump for c in range(3)]
                else:
                    tau = tau + absorb[k] * bump
                    emits = [emits[c] + shine[c][k] * bump for c in range(3)]
            series = tau * ((-1.0) ** (terms - 1) / math.factorial(terms))
            for n in range(terms - 1, 0, -1):
                series = (series + (-1.0) ** (n - 1) / math.factorial(n)) * tau
            for i in range(unroll):
                weight = trans * series[i]
                trans = trans - weight
                red = red + weight * emits[0][i]
                green = green + weight * emits[1][i]
                blue = blue + weight * emits[2][i]
            return trans, red, green, blue

        none = jnp.zeros((row_block, columns), F32)
        trans, red, green, blue = lax.fori_loop(0, depth // unroll, body, (none + 1.0, none, none, none))
        return red, green, blue, trans

    for step in range(1, nz):
        peer = lax.rem(iz + step, nz)
        for c, plane in enumerate(render(peer)):
            sent[step - 1, c] = plane
        copy = remote(sent.at[step - 1], pieces.at[iz], image_send.at[step - 1], image_recv.at[iz], ix, peer)
        copy.start()
        copies.append((None, copy))
    for c, plane in enumerate(render(iz)):
        pieces[iz, c] = plane

    for step in range(1, nz):
        peer = lax.rem(iz + step, nz)
        remote(pieces.at[peer], pieces.at[peer], image_send.at[step - 1], image_recv.at[peer], ix, peer).wait_recv()

    color = [pieces[0, c] for c in range(3)]
    trans = pieces[0, 3]
    for n in range(1, nz):
        color = [color[c] + trans * pieces[n, c] for c in range(3)]
        trans = trans * pieces[n, 3]
    for c in range(3):
        out_ref[c] = color[c]
    out_ref[3] = trans

    for condition, copy in copies:
        if condition is None:
            copy.wait_send()
        else:
            pl.when(condition)(copy.wait_send)


def on_device(volume, centers, sharpness, extinction, colors):
    nx, nz = lax.axis_size("gx"), lax.axis_size("gz")
    depth, rows, columns = volume.shape
    groups = depth // (columns // PIECE)
    row_block = rows // nz
    bound = 3.0 * centers.shape[0] / (depth * nz)
    terms = 1
    while bound ** terms / math.factorial(terms + 1) > 2.0 ** -26:
        terms += 1
    left, main, edge = constants(rows, columns)
    smem = pl.BlockSpec(memory_space=pltpu.SMEM)
    vmem = pl.BlockSpec(memory_space=pltpu.VMEM)
    dma = pltpu.SemaphoreType.DMA
    slab = (rows, columns)
    return pl.pallas_call(
        functools.partial(kernel, nx, nz, terms),
        out_shape=jax.ShapeDtypeStruct((4, row_block, columns), F32),
        in_specs=[pl.BlockSpec(memory_space=pl.ANY)] + [smem] * 4 + [vmem] * 3,
        out_specs=vmem,
        scratch_shapes=[
            pltpu.VMEM((depth,) + slab, F32),
            pltpu.VMEM((groups,) + slab, F32),
            pltpu.VMEM((groups + 2,) + slab, F32),
            pltpu.VMEM((groups + 2,) + slab, F32),
            pltpu.VMEM((2, HALO) + slab, F32),
            pltpu.VMEM((depth + 2 * HALO,) + slab, F32),
            pltpu.VMEM((nz - 1, 4, row_block, columns), F32),
            pltpu.VMEM((nz, 4, row_block, columns), F32),
            dma((groups,)),
            dma((groups + 2,)), dma((groups + 2,)),
            dma((groups + 2,)), dma((groups + 2,)),
            dma((2,)), dma((2,)),
            dma((nz - 1,)), dma((nz,)),
        ],
        compiler_params=pltpu.CompilerParams(
            collective_id=0, has_side_effects=True, vmem_limit_bytes=32 * 1024 * 1024
        ),
    )(volume, centers, sharpness, extinction, colors, jnp.asarray(left), jnp.asarray(main), jnp.asarray(edge))


def solution(mesh):
    return jax.shard_map(
        on_device,
        mesh=mesh,
        in_specs=(P("gz", None, "gx"), P(), P(), P(), P()),
        out_specs=P(None, "gz", "gx"),
        check_vma=False,
    )
```

```python
import functools
import math

import jax
import jax.numpy as jnp
import numpy as np
from jax import lax
from jax.experimental import pallas as pl
from jax.experimental.pallas import tpu as pltpu
from jax.sharding import PartitionSpec as P

F32 = jnp.float32
BF16 = jnp.bfloat16
MESH = pl.DeviceIdType.MESH
HALO = 4


def tap_weights():
    raw = [math.exp(-(j * j) / 8.0) for j in range(-4, 5)]
    whole = sum(raw)
    return [value / whole for value in raw]


def split_const(matrix):
    high = matrix.astype(np.float32).astype(BF16)
    low = (matrix - high.astype(np.float64)).astype(np.float32).astype(BF16)
    return high, low


def band(count, shift, rows):
    weights = tap_weights()
    matrix = np.zeros((rows, count), np.float64)
    for source in range(rows):
        for target in range(count):
            offset = shift(source) - target
            if -4 <= offset <= 4:
                matrix[source, target] = weights[offset + 4]
    return matrix


def constants(rows, columns):
    high, low = split_const(band(rows, lambda i: i, rows).T)
    left = np.concatenate([high, high, low], axis=1)
    high, low = split_const(band(columns, lambda i: i, columns))
    main = np.concatenate([high, high, low], axis=0)
    side = band(columns, lambda i: i - HALO if i < HALO else columns + i - HALO, 2 * HALO)
    half = columns // 2
    edges = []
    for m in range(half // HALO):
        spot = np.zeros((columns, columns), np.float64)
        spot[HALO * m:HALO * (m + 1)] = side[:HALO]
        spot[half + HALO * m:half + HALO * (m + 1)] = side[HALO:]
        high, low = split_const(spot)
        edges.append(np.concatenate([high, high, low], axis=0))
    edge = np.stack([np.concatenate(edges[m:m + 2], axis=1) for m in range(0, len(edges), 2)])
    return left, main, edge


def split(value):
    high = value.astype(BF16)
    low = (value - high.astype(F32)).astype(BF16)
    return high, low


def rows_pass(left, slab):
    high, low = split(slab)
    return jnp.dot(left, jnp.concatenate([high, low, high], axis=0), preferred_element_type=F32)


def columns_pass(rows, matrix):
    high, low = split(rows)
    return jnp.dot(jnp.concatenate([high, low, high], axis=1), matrix, preferred_element_type=F32)


def kernel(nx, nz, terms, volume, centers_in, sharpness_in, extinction_in, colors_in, left_in, main_in, edge_in,
           out_ref, centers, sharpness, extinction, colors, left_ref, main_ref, edge_ref, vol, packed, corner,
           beside, corner_in, layers, tall_ref, smooth, sent, pieces, load_sem, small_sem,
           beside_send, beside_recv, corner_send, corner_recv, layer_send, layer_recv, image_send, image_recv):
    depth, rows, columns = vol.shape
    per_group = columns // HALO
    groups = depth // per_group
    half = columns // 2
    row_block = rows // nz
    ix = lax.axis_index("gx")
    iz = lax.axis_index("gz")
    sides = ((ix < nx - 1, ix + 1), (ix > 0, ix - 1))
    ends = ((iz > 0, iz - 1), (iz < nz - 1, iz + 1))

    loads = []
    chunk = per_group // 2
    for g in range(2 * groups):
        span = pl.ds(g * chunk, chunk)
        loads.append(pltpu.make_async_copy(volume.at[span], vol.at[span], load_sem.at[g]))
        loads[-1].start()

    barrier = pltpu.get_barrier_semaphore()

    def greet(x, z):
        pl.semaphore_signal(barrier, inc=1, device_id={"gx": x, "gz": z}, device_id_type=MESH)

    for here, x in sides:
        pl.when(here)(functools.partial(greet, x, iz))
        for there, z in ends:
            pl.when(here & there)(functools.partial(greet, x, z))
    for step in range(1, nz):
        greet(ix, lax.rem(iz + step, nz))

    smalls = []
    for i, (source, target) in enumerate((
        (left_in, left_ref), (main_in, main_ref), (edge_in, edge_ref), (centers_in, centers),
        (sharpness_in, sharpness), (extinction_in, extinction), (colors_in, colors),
    )):
        smalls.append(pltpu.make_async_copy(source, target, small_sem.at[i]))
        smalls[-1].start()

    lane = lax.broadcasted_iota(jnp.int32, (rows, columns), 1)
    lane8 = lax.broadcasted_iota(jnp.int32, (8, columns), 1)
    corner_lanes = HALO * HALO

    def remote(source, target, send, recv, x, z):
        return pltpu.make_async_remote_copy(
            src_ref=source, dst_ref=target, send_sem=send, recv_sem=recv,
            device_id={"gx": x, "gz": z}, device_id_type=MESH,
        )

    def arrival(target, send, recv):
        return remote(target, target, send, recv, ix, iz)

    copies = []

    def launch(condition, copy):
        copies.append((condition, copy))
        pl.when(condition)(copy.start)

    for g in range(groups):
        totals = [jnp.zeros((rows, columns), F32)] * 2
        for m in range(per_group):
            if m % chunk == 0:
                loads[(g * per_group + m) // chunk].wait()
            plane = vol[g * per_group + m]
            for side, shift in ((0, HALO * m + HALO), (1, HALO * m)):
                shift = shift % columns
                turned = pltpu.roll(plane, shift, axis=1) if shift else plane
                totals[side] = jnp.where(lane // HALO == m, turned, totals[side])
        for side in range(2):
            packed[side, g] = totals[side]
        if g == 0:
            count = nz - 1
            for here, x in sides:
                span = 1 + ends[0][0].astype(jnp.int32) + ends[1][0].astype(jnp.int32)
                count = count + here.astype(jnp.int32) * span
            pl.semaphore_wait(barrier, count)
        for side, (here, x) in enumerate(sides):
            launch(here, remote(packed.at[side, g], beside.at[side, g], beside_send.at[side, g], beside_recv.at[side, g], x, iz))
        if g == 0:
            for end, (there, z) in enumerate(ends):
                edge_span = pl.ds(0 if end == 0 else depth - HALO, HALO)
                launch(there, remote(volume.at[edge_span], layers.at[1 - end], layer_send.at[end], layer_recv.at[1 - end], ix, z))
        for end, (there, z) in enumerate(ends):
            if g != (0 if end == 0 else groups - 1):
                continue
            first = 0 if end == 0 else columns - corner_lanes
            for side, (here, x) in enumerate(sides):
                small = jnp.zeros((8, columns), F32)
                for t in range(rows // 8):
                    shift = (corner_lanes * t - first) % columns
                    turned = totals[side][8 * t:8 * t + 8]
                    turned = pltpu.roll(turned, shift, axis=1) if shift else turned
                    small = jnp.where(lane8 // corner_lanes == t, turned, small)
                corner[side, end] = small
                launch(here & there, remote(
                    corner.at[side, end], corner_in.at[side, 1 - end],
                    corner_send.at[side, end], corner_recv.at[side, 1 - end], x, z,
                ))

    for small in smalls:
        small.wait()
    left = left_ref[...]

    def plane_pass(source, start, target):
        wide = jnp.concatenate([source[start + i] for i in range(HALO)], axis=1)
        wide = rows_pass(left, wide)
        tall = jnp.concatenate([wide[:, i * columns:(i + 1) * columns] for i in range(HALO)], axis=0)
        tall = columns_pass(tall, main_ref[...])
        for i in range(HALO):
            smooth[target + i] = tall[i * rows:(i + 1) * rows]

    @pl.loop(0, depth // HALO)
    def _(step):
        plane_pass(vol, step * HALO, step * HALO + HALO)

    def arrive(condition, copy, inbox):
        pl.when(condition)(copy.wait_recv)

        @pl.when(jnp.logical_not(condition))
        def _():
            inbox[...] = jnp.zeros(inbox.shape, F32)

    for end, (there, z) in enumerate(ends):
        arrive(there, arrival(layers.at[end], layer_send.at[end], layer_recv.at[end]), layers.at[end])
        plane_pass(layers.at[end], 0, end * (depth + HALO))

    for side in range(2):
        here = sides[1 - side][0]
        for g in range(groups):
            slot = (side, g)
            arrive(here, arrival(beside.at[slot], beside_send.at[slot], beside_recv.at[slot]), beside.at[slot])
        for end, (there, z) in enumerate(ends):
            slot = (side, end)
            arrive(here & there, arrival(corner_in.at[slot], corner_send.at[slot], corner_recv.at[slot]), corner_in.at[slot])

    blocks = []
    for g in range(groups):
        near, far = beside[0, g], beside[1, g]
        blocks.append(jnp.where(lane < half, near, pltpu.roll(far, half, axis=1)))
        blocks.append(jnp.where(lane < half, pltpu.roll(near, half, axis=1), far))
    for end in range(2):
        spread = []
        for t in range(rows // 8):
            shift = (columns - corner_lanes * t) % columns
            near = pltpu.roll(corner_in[0, end], shift, axis=1) if shift else corner_in[0, end]
            shift = (columns + half - corner_lanes * t) % columns
            far = pltpu.roll(corner_in[1, end], shift, axis=1) if shift else corner_in[1, end]
            spread.append(jnp.where(lane8 < half, near, far))
        blocks.append(jnp.concatenate(spread, axis=0))
    wide = rows_pass(left, jnp.concatenate(blocks, axis=1))
    high, low = split(jnp.concatenate([wide[:, i * columns:(i + 1) * columns] for i in range(len(blocks))], axis=0))
    tall_ref[...] = jnp.concatenate([high, low, high], axis=1)
    per_block = half // HALO

    def edges(pair, block, count, places):
        part = jnp.dot(tall_ref[block * rows:(block + count) * rows], edge_ref[pair], preferred_element_type=F32)
        for p, place in enumerate(places):
            for i in range(2):
                smooth[place + i] += part[p * rows:(p + 1) * rows, i * columns:(i + 1) * columns]

    for pair in range(HALO // 2):
        edges(pair, 2 * groups, 2, [2 * pair, depth + HALO + 2 * pair])

    @pl.loop(0, per_block // 2)
    def _(pair):
        edges(pair, 0, 2 * groups, [HALO + p * per_block + 2 * pair for p in range(2 * groups)])

    taps = tap_weights()
    comps = centers.shape[0]
    cells = depth * nz
    middle = [centers[k] for k in range(comps)]
    fall = [-sharpness[k] for k in range(comps)]
    absorb = [extinction[k] * F32(1.0 / cells) for k in range(comps)]
    shine = [[colors[c, k] for k in range(comps)] for c in range(3)]
    unroll = 2

    def render(row):
        start = pl.multiple_of(row * row_block, row_block)

        def body(step, carry):
            trans, red, green, blue = carry
            z = step * unroll

            def load(j):
                return smooth[pl.ds(z + j, unroll), pl.ds(start, row_block), :]

            density = taps[4] * load(4)
            for j in range(4):
                density = density + taps[j] * (load(j) + load(8 - j))
            tau = None
            for k in range(comps):
                offset = density - middle[k]
                bump = jnp.exp(fall[k] * offset * offset)
                if tau is None:
                    tau = absorb[k] * bump
                    emits = [shine[c][k] * bump for c in range(3)]
                else:
                    tau = tau + absorb[k] * bump
                    emits = [emits[c] + shine[c][k] * bump for c in range(3)]
            series = tau * ((-1.0) ** (terms - 1) / math.factorial(terms))
            for n in range(terms - 1, 0, -1):
                series = (series + (-1.0) ** (n - 1) / math.factorial(n)) * tau
            for i in range(unroll):
                weight = trans * series[i]
                trans = trans - weight
                red = red + weight * emits[0][i]
                green = green + weight * emits[1][i]
                blue = blue + weight * emits[2][i]
            return trans, red, green, blue

        none = jnp.zeros((row_block, columns), F32)
        trans, red, green, blue = lax.fori_loop(0, depth // unroll, body, (none + 1.0, none, none, none))
        return red, green, blue, trans

    for step in range(1, nz):
        peer = lax.rem(iz + step, nz)
        for c, plane in enumerate(render(peer)):
            sent[step - 1, c] = plane
        copy = remote(sent.at[step - 1], pieces.at[iz], image_send.at[step - 1], image_recv.at[iz], ix, peer)
        copy.start()
        copies.append((None, copy))
    for c, plane in enumerate(render(iz)):
        pieces[iz, c] = plane

    for step in range(1, nz):
        peer = lax.rem(iz + step, nz)
        remote(pieces.at[peer], pieces.at[peer], image_send.at[step - 1], image_recv.at[peer], ix, peer).wait_recv()

    color = [pieces[0, c] for c in range(3)]
    trans = pieces[0, 3]
    for n in range(1, nz):
        color = [color[c] + trans * pieces[n, c] for c in range(3)]
        trans = trans * pieces[n, 3]
    for c in range(3):
        out_ref[c] = color[c]
    out_ref[3] = trans

    for condition, copy in copies:
        if condition is None:
            copy.wait_send()
        else:
            pl.when(condition)(copy.wait_send)


def on_device(volume, centers, sharpness, extinction, colors):
    nx, nz = lax.axis_size("gx"), lax.axis_size("gz")
    depth, rows, columns = volume.shape
    groups = depth // (columns // HALO)
    row_block = rows // nz
    bound = 3.0 * centers.shape[0] / (depth * nz)
    terms = 1
    while bound ** terms / math.factorial(terms + 1) > 2.0 ** -26:
        terms += 1
    left, main, edge = constants(rows, columns)
    dma = pltpu.SemaphoreType.DMA
    slab = (rows, columns)
    return pl.pallas_call(
        functools.partial(kernel, nx, nz, terms),
        out_shape=jax.ShapeDtypeStruct((4, row_block, columns), F32),
        in_specs=[pl.BlockSpec(memory_space=pltpu.HBM)] * 8,
        out_specs=pl.BlockSpec(memory_space=pltpu.VMEM),
        scratch_shapes=[
            pltpu.SMEM(centers.shape, F32),
            pltpu.SMEM(sharpness.shape, F32),
            pltpu.SMEM(extinction.shape, F32),
            pltpu.SMEM(colors.shape, F32),
            pltpu.VMEM(left.shape, BF16),
            pltpu.VMEM(main.shape, BF16),
            pltpu.VMEM(edge.shape, BF16),
            pltpu.VMEM((depth,) + slab, F32),
            pltpu.VMEM((2, groups) + slab, F32),
            pltpu.VMEM((2, 2, 8, columns), F32),
            pltpu.VMEM((2, groups) + slab, F32),
            pltpu.VMEM((2, 2, 8, columns), F32),
            pltpu.VMEM((2, HALO) + slab, F32),
            pltpu.VMEM(((2 * groups + 2) * rows, 3 * columns), BF16),
            pltpu.VMEM((depth + 2 * HALO,) + slab, F32),
            pltpu.VMEM((nz - 1, 4, row_block, columns), F32),
            pltpu.VMEM((nz, 4, row_block, columns), F32),
            dma((2 * groups,)), dma((7,)),
            dma((2, groups)), dma((2, groups)),
            dma((2, 2)), dma((2, 2)),
            dma((2,)), dma((2,)),
            dma((nz - 1,)), dma((nz,)),
        ],
        compiler_params=pltpu.CompilerParams(
            collective_id=0, has_side_effects=True, vmem_limit_bytes=60 * 1024 * 1024
        ),
    )(volume, centers, sharpness, extinction, colors, jnp.asarray(left), jnp.asarray(main), jnp.asarray(edge))


def solution(mesh):
    return jax.shard_map(
        on_device,
        mesh=mesh,
        in_specs=(P("gz", None, "gx"), P(), P(), P(), P()),
        out_specs=P(None, "gz", "gx"),
        check_vma=False,
    )
```

```python
import functools
import math

import jax
import jax.numpy as jnp
import numpy as np
from jax import lax
from jax.experimental import pallas as pl
from jax.experimental.pallas import tpu as pltpu
from jax.sharding import PartitionSpec as P

F32 = jnp.float32
BF16 = jnp.bfloat16
MESH = pl.DeviceIdType.MESH
HALO = 4


def tap_weights():
    raw = [math.exp(-(j * j) / 8.0) for j in range(-4, 5)]
    whole = sum(raw)
    return [value / whole for value in raw]


def split_const(matrix):
    high = matrix.astype(np.float32).astype(BF16)
    low = (matrix - high.astype(np.float64)).astype(np.float32).astype(BF16)
    return high, low


def band(count, shift, rows):
    weights = tap_weights()
    matrix = np.zeros((rows, count), np.float64)
    for source in range(rows):
        for target in range(count):
            offset = shift(source) - target
            if -4 <= offset <= 4:
                matrix[source, target] = weights[offset + 4]
    return matrix


def constants(rows, columns):
    high, low = split_const(band(rows, lambda i: i, rows).T)
    left = np.concatenate([high, high, low], axis=1)
    high, low = split_const(band(columns, lambda i: i, columns))
    main = np.concatenate([np.concatenate([high, high], axis=0), np.concatenate([low, low], axis=0)], axis=1)
    side = band(columns, lambda i: i - HALO if i < HALO else columns + i - HALO, 2 * HALO)
    half = columns // 2
    edges = []
    for m in range(half // HALO):
        spot = np.zeros((columns, columns), np.float64)
        spot[HALO * m:HALO * (m + 1)] = side[:HALO]
        spot[half + HALO * m:half + HALO * (m + 1)] = side[HALO:]
        high, low = split_const(spot)
        edges.append(np.concatenate([high, high, low], axis=0))
    edge = np.stack([np.concatenate(edges[m:m + 2], axis=1) for m in range(0, len(edges), 2)])
    return left, main, edge


def split(value):
    high = value.astype(BF16)
    low = (value - high.astype(F32)).astype(BF16)
    return high, low


def rows_pass(left, slab):
    high, low = split(slab)
    return jnp.dot(left, jnp.concatenate([high, low, high], axis=0), preferred_element_type=F32)


def columns_pass(rows, matrix):
    high, low = split(rows)
    both = jnp.dot(jnp.concatenate([high, low], axis=1), matrix, preferred_element_type=F32)
    count = both.shape[1] // 2
    return both[:, :count] + both[:, count:]


def kernel(nx, nz, terms, volume, centers_in, sharpness_in, extinction_in, colors_in, left_in, main_in, edge_in,
           out_ref, centers, sharpness, extinction, colors, left_ref, main_ref, edge_ref, vol, packed, corner,
           beside, corner_in, layers, tall_ref, smooth, sent, pieces, load_sem, small_sem,
           beside_send, beside_recv, corner_send, corner_recv, layer_send, layer_recv, image_send, image_recv):
    depth, rows, columns = vol.shape
    per_group = columns // HALO
    groups = depth // per_group
    half = columns // 2
    row_block = rows // nz
    ix = lax.axis_index("gx")
    iz = lax.axis_index("gz")
    sides = ((ix < nx - 1, ix + 1), (ix > 0, ix - 1))
    ends = ((iz > 0, iz - 1), (iz < nz - 1, iz + 1))

    loads = []
    chunk = per_group // 2
    for g in range(2 * groups):
        span = pl.ds(g * chunk, chunk)
        loads.append(pltpu.make_async_copy(volume.at[span], vol.at[span], load_sem.at[g]))
        loads[-1].start()

    barrier = pltpu.get_barrier_semaphore()

    def greet(x, z):
        pl.semaphore_signal(barrier, inc=1, device_id={"gx": x, "gz": z}, device_id_type=MESH)

    for here, x in sides:
        pl.when(here)(functools.partial(greet, x, iz))
        for there, z in ends:
            pl.when(here & there)(functools.partial(greet, x, z))
    for step in range(1, nz):
        greet(ix, lax.rem(iz + step, nz))

    smalls = []
    for i, (source, target) in enumerate((
        (left_in, left_ref), (main_in, main_ref), (edge_in, edge_ref), (centers_in, centers),
        (sharpness_in, sharpness), (extinction_in, extinction), (colors_in, colors),
    )):
        smalls.append(pltpu.make_async_copy(source, target, small_sem.at[i]))
        smalls[-1].start()

    lane = lax.broadcasted_iota(jnp.int32, (rows, columns), 1)
    lane8 = lax.broadcasted_iota(jnp.int32, (8, columns), 1)
    corner_lanes = HALO * HALO

    def remote(source, target, send, recv, x, z):
        return pltpu.make_async_remote_copy(
            src_ref=source, dst_ref=target, send_sem=send, recv_sem=recv,
            device_id={"gx": x, "gz": z}, device_id_type=MESH,
        )

    def arrival(target, send, recv):
        return remote(target, target, send, recv, ix, iz)

    copies = []

    def launch(condition, copy):
        copies.append((condition, copy))
        pl.when(condition)(copy.start)

    for g in range(groups):
        totals = [jnp.zeros((rows, columns), F32)] * 2
        for m in range(per_group):
            if m % chunk == 0:
                loads[(g * per_group + m) // chunk].wait()
            plane = vol[g * per_group + m]
            for side, shift in ((0, HALO * m + HALO), (1, HALO * m)):
                shift = shift % columns
                turned = pltpu.roll(plane, shift, axis=1) if shift else plane
                totals[side] = jnp.where(lane // HALO == m, turned, totals[side])
        for side in range(2):
            packed[side, g] = totals[side]
        if g == 0:
            count = nz - 1
            for here, x in sides:
                span = 1 + ends[0][0].astype(jnp.int32) + ends[1][0].astype(jnp.int32)
                count = count + here.astype(jnp.int32) * span
            pl.semaphore_wait(barrier, count)
        for side, (here, x) in enumerate(sides):
            launch(here, remote(packed.at[side, g], beside.at[side, g], beside_send.at[side, g], beside_recv.at[side, g], x, iz))
        if g == 0:
            for end, (there, z) in enumerate(ends):
                edge_span = pl.ds(0 if end == 0 else depth - HALO, HALO)
                launch(there, remote(volume.at[edge_span], layers.at[1 - end], layer_send.at[end], layer_recv.at[1 - end], ix, z))
        for end, (there, z) in enumerate(ends):
            if g != (0 if end == 0 else groups - 1):
                continue
            first = 0 if end == 0 else columns - corner_lanes
            for side, (here, x) in enumerate(sides):
                small = jnp.zeros((8, columns), F32)
                for t in range(rows // 8):
                    shift = (corner_lanes * t - first) % columns
                    turned = totals[side][8 * t:8 * t + 8]
                    turned = pltpu.roll(turned, shift, axis=1) if shift else turned
                    small = jnp.where(lane8 // corner_lanes == t, turned, small)
                corner[side, end] = small
                launch(here & there, remote(
                    corner.at[side, end], corner_in.at[side, 1 - end],
                    corner_send.at[side, end], corner_recv.at[side, 1 - end], x, z,
                ))

    for small in smalls:
        small.wait()
    left = left_ref[...]

    def plane_pass(source, start, target):
        wide = jnp.concatenate([source[start + i] for i in range(HALO)], axis=1)
        wide = rows_pass(left, wide)
        tall = jnp.concatenate([wide[:, i * columns:(i + 1) * columns] for i in range(HALO)], axis=0)
        tall = columns_pass(tall, main_ref[...])
        for i in range(HALO):
            smooth[target + i] = tall[i * rows:(i + 1) * rows]

    @pl.loop(0, depth // HALO, unroll=8)
    def _(step):
        plane_pass(vol, step * HALO, step * HALO + HALO)

    def arrive(condition, copy, inbox):
        pl.when(condition)(copy.wait_recv)

        @pl.when(jnp.logical_not(condition))
        def _():
            inbox[...] = jnp.zeros(inbox.shape, F32)

    for end, (there, z) in enumerate(ends):
        arrive(there, arrival(layers.at[end], layer_send.at[end], layer_recv.at[end]), layers.at[end])
        plane_pass(layers.at[end], 0, end * (depth + HALO))

    for side in range(2):
        here = sides[1 - side][0]
        for g in range(groups):
            slot = (side, g)
            arrive(here, arrival(beside.at[slot], beside_send.at[slot], beside_recv.at[slot]), beside.at[slot])
        for end, (there, z) in enumerate(ends):
            slot = (side, end)
            arrive(here & there, arrival(corner_in.at[slot], corner_send.at[slot], corner_recv.at[slot]), corner_in.at[slot])

    blocks = []
    for g in range(groups):
        near, far = beside[0, g], beside[1, g]
        blocks.append(jnp.where(lane < half, near, pltpu.roll(far, half, axis=1)))
        blocks.append(jnp.where(lane < half, pltpu.roll(near, half, axis=1), far))
    for end in range(2):
        spread = []
        for t in range(rows // 8):
            shift = (columns - corner_lanes * t) % columns
            near = pltpu.roll(corner_in[0, end], shift, axis=1) if shift else corner_in[0, end]
            shift = (columns + half - corner_lanes * t) % columns
            far = pltpu.roll(corner_in[1, end], shift, axis=1) if shift else corner_in[1, end]
            spread.append(jnp.where(lane8 < half, near, far))
        blocks.append(jnp.concatenate(spread, axis=0))
    wide = rows_pass(left, jnp.concatenate(blocks, axis=1))
    high, low = split(jnp.concatenate([wide[:, i * columns:(i + 1) * columns] for i in range(len(blocks))], axis=0))
    tall_ref[...] = jnp.concatenate([high, low, high], axis=1)
    per_block = half // HALO

    def edges(pair, block, count, places):
        part = jnp.dot(tall_ref[block * rows:(block + count) * rows], edge_ref[pair], preferred_element_type=F32)
        for p, place in enumerate(places):
            for i in range(2):
                smooth[place + i] += part[p * rows:(p + 1) * rows, i * columns:(i + 1) * columns]

    for pair in range(HALO // 2):
        edges(pair, 2 * groups, 2, [2 * pair, depth + HALO + 2 * pair])

    @pl.loop(0, per_block // 2, unroll=8)
    def _(pair):
        edges(pair, 0, 2 * groups, [HALO + p * per_block + 2 * pair for p in range(2 * groups)])

    taps = tap_weights()
    comps = centers.shape[0]
    cells = depth * nz
    middle = [centers[k] for k in range(comps)]
    fall = [-sharpness[k] for k in range(comps)]
    absorb = [extinction[k] * F32(1.0 / cells) for k in range(comps)]
    shine = [[colors[c, k] for k in range(comps)] for c in range(3)]
    unroll = 4

    def render(row):
        start = pl.multiple_of(row * row_block, row_block)

        def body(step, carry):
            trans, red, green, blue = carry
            z = step * unroll

            def load(j):
                return smooth[pl.ds(z + j, unroll), pl.ds(start, row_block), :]

            density = taps[4] * load(4)
            for j in range(4):
                density = density + taps[j] * (load(j) + load(8 - j))
            tau = None
            for k in range(comps):
                offset = density - middle[k]
                bump = jnp.exp(fall[k] * offset * offset)
                if tau is None:
                    tau = absorb[k] * bump
                    emits = [shine[c][k] * bump for c in range(3)]
                else:
                    tau = tau + absorb[k] * bump
                    emits = [emits[c] + shine[c][k] * bump for c in range(3)]
            series = tau * ((-1.0) ** (terms - 1) / math.factorial(terms))
            for n in range(terms - 1, 0, -1):
                series = (series + (-1.0) ** (n - 1) / math.factorial(n)) * tau
            for i in range(unroll):
                weight = trans * series[i]
                trans = trans - weight
                red = red + weight * emits[0][i]
                green = green + weight * emits[1][i]
                blue = blue + weight * emits[2][i]
            return trans, red, green, blue

        none = jnp.zeros((row_block, columns), F32)
        trans, red, green, blue = lax.fori_loop(0, depth // unroll, body, (none + 1.0, none, none, none))
        return red, green, blue, trans

    for step in range(1, nz):
        peer = lax.rem(iz + step, nz)
        for c, plane in enumerate(render(peer)):
            sent[step - 1, c] = plane
        copy = remote(sent.at[step - 1], pieces.at[iz], image_send.at[step - 1], image_recv.at[iz], ix, peer)
        copy.start()
        copies.append((None, copy))
    for c, plane in enumerate(render(iz)):
        pieces[iz, c] = plane

    for step in range(1, nz):
        peer = lax.rem(iz + step, nz)
        remote(pieces.at[peer], pieces.at[peer], image_send.at[step - 1], image_recv.at[peer], ix, peer).wait_recv()

    color = [pieces[0, c] for c in range(3)]
    trans = pieces[0, 3]
    for n in range(1, nz):
        color = [color[c] + trans * pieces[n, c] for c in range(3)]
        trans = trans * pieces[n, 3]
    for c in range(3):
        out_ref[c] = color[c]
    out_ref[3] = trans

    for condition, copy in copies:
        if condition is None:
            copy.wait_send()
        else:
            pl.when(condition)(copy.wait_send)


def on_device(volume, centers, sharpness, extinction, colors):
    nx, nz = lax.axis_size("gx"), lax.axis_size("gz")
    depth, rows, columns = volume.shape
    groups = depth // (columns // HALO)
    row_block = rows // nz
    bound = 3.0 * centers.shape[0] / (depth * nz)
    terms = 1
    while bound ** terms / math.factorial(terms + 1) > 2.0 ** -26:
        terms += 1
    left, main, edge = constants(rows, columns)
    dma = pltpu.SemaphoreType.DMA
    slab = (rows, columns)
    return pl.pallas_call(
        functools.partial(kernel, nx, nz, terms),
        out_shape=jax.ShapeDtypeStruct((4, row_block, columns), F32),
        in_specs=[pl.BlockSpec(memory_space=pltpu.HBM)] * 8,
        out_specs=pl.BlockSpec(memory_space=pltpu.VMEM),
        scratch_shapes=[
            pltpu.SMEM(centers.shape, F32),
            pltpu.SMEM(sharpness.shape, F32),
            pltpu.SMEM(extinction.shape, F32),
            pltpu.SMEM(colors.shape, F32),
            pltpu.VMEM(left.shape, BF16),
            pltpu.VMEM(main.shape, BF16),
            pltpu.VMEM(edge.shape, BF16),
            pltpu.VMEM((depth,) + slab, F32),
            pltpu.VMEM((2, groups) + slab, F32),
            pltpu.VMEM((2, 2, 8, columns), F32),
            pltpu.VMEM((2, groups) + slab, F32),
            pltpu.VMEM((2, 2, 8, columns), F32),
            pltpu.VMEM((2, HALO) + slab, F32),
            pltpu.VMEM(((2 * groups + 2) * rows, 3 * columns), BF16),
            pltpu.VMEM((depth + 2 * HALO,) + slab, F32),
            pltpu.VMEM((nz - 1, 4, row_block, columns), F32),
            pltpu.VMEM((nz, 4, row_block, columns), F32),
            dma((2 * groups,)), dma((7,)),
            dma((2, groups)), dma((2, groups)),
            dma((2, 2)), dma((2, 2)),
            dma((2,)), dma((2,)),
            dma((nz - 1,)), dma((nz,)),
        ],
        compiler_params=pltpu.CompilerParams(
            collective_id=0, has_side_effects=True, vmem_limit_bytes=60 * 1024 * 1024
        ),
    )(volume, centers, sharpness, extinction, colors, jnp.asarray(left), jnp.asarray(main), jnp.asarray(edge))


def solution(mesh):
    return jax.shard_map(
        on_device,
        mesh=mesh,
        in_specs=(P("gz", None, "gx"), P(), P(), P(), P()),
        out_specs=P(None, "gz", "gx"),
        check_vma=False,
    )
```

```python
import functools
import math

import jax
import jax.numpy as jnp
import numpy as np
from jax import lax
from jax.experimental import pallas as pl
from jax.experimental.pallas import tpu as pltpu
from jax.sharding import PartitionSpec as P

F32 = jnp.float32
BF16 = jnp.bfloat16
MESH = pl.DeviceIdType.MESH
HALO = 4


def tap_weights():
    raw = [math.exp(-(j * j) / 8.0) for j in range(-4, 5)]
    whole = sum(raw)
    return [value / whole for value in raw]


def split_const(matrix):
    high = matrix.astype(np.float32).astype(BF16)
    low = (matrix - high.astype(np.float64)).astype(np.float32).astype(BF16)
    return high, low


def band(count, shift, rows):
    weights = tap_weights()
    matrix = np.zeros((rows, count), np.float64)
    for source in range(rows):
        for target in range(count):
            offset = shift(source) - target
            if -4 <= offset <= 4:
                matrix[source, target] = weights[offset + 4]
    return matrix


def constants(rows, columns):
    high, low = split_const(band(rows, lambda i: i, rows).T)
    left = np.concatenate([high, high, low], axis=1)
    high, low = split_const(band(columns, lambda i: i, columns))
    main = np.concatenate([np.concatenate([high, high], axis=0), np.concatenate([low, low], axis=0)], axis=1)
    side = band(columns, lambda i: i - HALO if i < HALO else columns + i - HALO, 2 * HALO)
    half = columns // 2
    edges = []
    for m in range(half // HALO):
        spot = np.zeros((columns, columns), np.float64)
        spot[HALO * m:HALO * (m + 1)] = side[:HALO]
        spot[half + HALO * m:half + HALO * (m + 1)] = side[HALO:]
        high, low = split_const(spot)
        edges.append(np.concatenate([high, high, low], axis=0))
    edge = np.stack([np.concatenate(edges[m:m + 2], axis=1) for m in range(0, len(edges), 2)])
    return left, main, edge


def split(value):
    high = value.astype(BF16)
    low = (value - high.astype(F32)).astype(BF16)
    return high, low


def rows_pass(left, slab):
    high, low = split(slab)
    return jnp.dot(left, jnp.concatenate([high, low, high], axis=0), preferred_element_type=F32)


def columns_pass(rows, matrix):
    high, low = split(rows)
    both = jnp.dot(jnp.concatenate([high, low], axis=1), matrix, preferred_element_type=F32)
    count = both.shape[1] // 2
    return both[:, :count] + both[:, count:]


def kernel(nx, nz, terms, volume, centers_in, sharpness_in, extinction_in, colors_in, left_in, main_in, edge_in,
           out_ref, centers, sharpness, extinction, colors, left_ref, main_ref, edge_ref, vol, packed, corner,
           beside, corner_in, layers, tall_ref, smooth, sent, pieces, load_sem, small_sem,
           beside_send, beside_recv, corner_send, corner_recv, layer_send, layer_recv, image_send, image_recv):
    depth, rows, columns = vol.shape
    per_group = columns // HALO
    groups = depth // per_group
    half = columns // 2
    row_block = rows // nz
    ix = lax.axis_index("gx")
    iz = lax.axis_index("gz")
    sides = ((ix < nx - 1, ix + 1), (ix > 0, ix - 1))
    ends = ((iz > 0, iz - 1), (iz < nz - 1, iz + 1))

    barrier = pltpu.get_barrier_semaphore()

    def greet(x, z):
        pl.semaphore_signal(barrier, inc=1, device_id={"gx": x, "gz": z}, device_id_type=MESH)

    for here, x in sides:
        pl.when(here)(functools.partial(greet, x, iz))
        for there, z in ends:
            pl.when(here & there)(functools.partial(greet, x, z))
    for step in range(1, nz):
        greet(ix, lax.rem(iz + step, nz))

    loads = []
    chunk = per_group // 2
    for g in range(2 * groups):
        span = pl.ds(g * chunk, chunk)
        loads.append(pltpu.make_async_copy(volume.at[span], vol.at[span], load_sem.at[g]))
        loads[-1].start()

    smalls = []
    for i, (source, target) in enumerate((
        (left_in, left_ref), (main_in, main_ref), (edge_in, edge_ref), (centers_in, centers),
        (sharpness_in, sharpness), (extinction_in, extinction), (colors_in, colors),
    )):
        smalls.append(pltpu.make_async_copy(source, target, small_sem.at[i]))
        smalls[-1].start()

    lane = lax.broadcasted_iota(jnp.int32, (rows, columns), 1)
    lane8 = lax.broadcasted_iota(jnp.int32, (8, columns), 1)
    corner_lanes = HALO * HALO

    def remote(source, target, send, recv, x, z):
        return pltpu.make_async_remote_copy(
            src_ref=source, dst_ref=target, send_sem=send, recv_sem=recv,
            device_id={"gx": x, "gz": z}, device_id_type=MESH,
        )

    def arrival(target, send, recv):
        return remote(target, target, send, recv, ix, iz)

    copies = []

    def launch(condition, copy):
        copies.append((condition, copy))
        pl.when(condition)(copy.start)

    for g in range(groups):
        totals = [jnp.zeros((rows, columns), F32)] * 2
        for m in range(per_group):
            if m % chunk == 0:
                loads[(g * per_group + m) // chunk].wait()
            plane = vol[g * per_group + m]
            for side, shift in ((0, HALO * m + HALO), (1, HALO * m)):
                shift = shift % columns
                turned = pltpu.roll(plane, shift, axis=1) if shift else plane
                totals[side] = jnp.where(lane // HALO == m, turned, totals[side])
        for side in range(2):
            packed[side, g] = totals[side]
        if g == 0:
            count = nz - 1
            for here, x in sides:
                span = 1 + ends[0][0].astype(jnp.int32) + ends[1][0].astype(jnp.int32)
                count = count + here.astype(jnp.int32) * span
            pl.semaphore_wait(barrier, count)
        for side, (here, x) in enumerate(sides):
            launch(here, remote(packed.at[side, g], beside.at[side, g], beside_send.at[side, g], beside_recv.at[side, g], x, iz))
        if g == 0:
            for end, (there, z) in enumerate(ends):
                edge_span = pl.ds(0 if end == 0 else depth - HALO, HALO)
                launch(there, remote(volume.at[edge_span], layers.at[1 - end], layer_send.at[end], layer_recv.at[1 - end], ix, z))
        for end, (there, z) in enumerate(ends):
            if g != (0 if end == 0 else groups - 1):
                continue
            first = 0 if end == 0 else columns - corner_lanes
            for side, (here, x) in enumerate(sides):
                small = jnp.zeros((8, columns), F32)
                for t in range(rows // 8):
                    shift = (corner_lanes * t - first) % columns
                    turned = totals[side][8 * t:8 * t + 8]
                    turned = pltpu.roll(turned, shift, axis=1) if shift else turned
                    small = jnp.where(lane8 // corner_lanes == t, turned, small)
                corner[side, end] = small
                launch(here & there, remote(
                    corner.at[side, end], corner_in.at[side, 1 - end],
                    corner_send.at[side, end], corner_recv.at[side, 1 - end], x, z,
                ))

    for small in smalls:
        small.wait()
    left = left_ref[...]

    def plane_pass(source, start, target):
        wide = jnp.concatenate([source[start + i] for i in range(HALO)], axis=1)
        wide = rows_pass(left, wide)
        tall = jnp.concatenate([wide[:, i * columns:(i + 1) * columns] for i in range(HALO)], axis=0)
        tall = columns_pass(tall, main_ref[...])
        for i in range(HALO):
            smooth[target + i] = tall[i * rows:(i + 1) * rows]

    @pl.loop(0, depth // HALO, unroll=8)
    def _(step):
        plane_pass(vol, step * HALO, step * HALO + HALO)

    def arrive(condition, copy, inbox):
        pl.when(condition)(copy.wait_recv)

        @pl.when(jnp.logical_not(condition))
        def _():
            inbox[...] = jnp.zeros(inbox.shape, F32)

    for end, (there, z) in enumerate(ends):
        arrive(there, arrival(layers.at[end], layer_send.at[end], layer_recv.at[end]), layers.at[end])
        plane_pass(layers.at[end], 0, end * (depth + HALO))

    for side in range(2):
        here = sides[1 - side][0]
        for g in range(groups):
            slot = (side, g)
            arrive(here, arrival(beside.at[slot], beside_send.at[slot], beside_recv.at[slot]), beside.at[slot])
        for end, (there, z) in enumerate(ends):
            slot = (side, end)
            arrive(here & there, arrival(corner_in.at[slot], corner_send.at[slot], corner_recv.at[slot]), corner_in.at[slot])

    blocks = []
    for g in range(groups):
        near, far = beside[0, g], beside[1, g]
        blocks.append(jnp.where(lane < half, near, pltpu.roll(far, half, axis=1)))
        blocks.append(jnp.where(lane < half, pltpu.roll(near, half, axis=1), far))
    for end in range(2):
        spread = []
        for t in range(rows // 8):
            shift = (columns - corner_lanes * t) % columns
            near = pltpu.roll(corner_in[0, end], shift, axis=1) if shift else corner_in[0, end]
            shift = (columns + half - corner_lanes * t) % columns
            far = pltpu.roll(corner_in[1, end], shift, axis=1) if shift else corner_in[1, end]
            spread.append(jnp.where(lane8 < half, near, far))
        blocks.append(jnp.concatenate(spread, axis=0))
    wide = rows_pass(left, jnp.concatenate(blocks, axis=1))
    high, low = split(jnp.concatenate([wide[:, i * columns:(i + 1) * columns] for i in range(len(blocks))], axis=0))
    tall_ref[...] = jnp.concatenate([high, low, high], axis=1)
    per_block = half // HALO

    def edges(pair, block, count, places):
        part = jnp.dot(tall_ref[block * rows:(block + count) * rows], edge_ref[pair], preferred_element_type=F32)
        for p, place in enumerate(places):
            for i in range(2):
                smooth[place + i] += part[p * rows:(p + 1) * rows, i * columns:(i + 1) * columns]

    for pair in range(HALO // 2):
        edges(pair, 2 * groups, 2, [2 * pair, depth + HALO + 2 * pair])

    @pl.loop(0, per_block // 2, unroll=8)
    def _(pair):
        edges(pair, 0, 2 * groups, [HALO + p * per_block + 2 * pair for p in range(2 * groups)])

    taps = tap_weights()
    comps = centers.shape[0]
    cells = depth * nz
    middle = [centers[k] for k in range(comps)]
    fall = [sharpness[k] * F32(-math.log2(math.e)) for k in range(comps)]
    absorb = [extinction[k] * F32(1.0 / cells) for k in range(comps)]
    shine = [[colors[c, k] for k in range(comps)] for c in range(3)]
    unroll = 4

    def render(row):
        start = pl.multiple_of(row * row_block, row_block)

        def body(step, carry):
            trans, red, green, blue = carry
            z = step * unroll

            def load(j):
                return smooth[pl.ds(z + j, unroll), pl.ds(start, row_block), :]

            density = taps[4] * load(4)
            for j in range(4):
                density = density + taps[j] * (load(j) + load(8 - j))
            tau = None
            for k in range(comps):
                offset = density - middle[k]
                bump = jnp.exp2(fall[k] * offset * offset)
                if tau is None:
                    tau = absorb[k] * bump
                    emits = [shine[c][k] * bump for c in range(3)]
                else:
                    tau = tau + absorb[k] * bump
                    emits = [emits[c] + shine[c][k] * bump for c in range(3)]
            series = tau * ((-1.0) ** (terms - 1) / math.factorial(terms))
            for n in range(terms - 1, 0, -1):
                series = (series + (-1.0) ** (n - 1) / math.factorial(n)) * tau
            for i in range(unroll):
                weight = trans * series[i]
                trans = trans - weight
                red = red + weight * emits[0][i]
                green = green + weight * emits[1][i]
                blue = blue + weight * emits[2][i]
            return trans, red, green, blue

        none = jnp.zeros((row_block, columns), F32)
        trans, red, green, blue = lax.fori_loop(0, depth // unroll, body, (none + 1.0, none, none, none))
        return red, green, blue, trans

    for step in range(1, nz):
        peer = lax.rem(iz + step, nz)
        for c, plane in enumerate(render(peer)):
            sent[step - 1, c] = plane
        copy = remote(sent.at[step - 1], pieces.at[iz], image_send.at[step - 1], image_recv.at[iz], ix, peer)
        copy.start()
        copies.append((None, copy))
    for c, plane in enumerate(render(iz)):
        pieces[iz, c] = plane

    for step in range(1, nz):
        peer = lax.rem(iz + step, nz)
        remote(pieces.at[peer], pieces.at[peer], image_send.at[step - 1], image_recv.at[peer], ix, peer).wait_recv()

    color = [pieces[0, c] for c in range(3)]
    trans = pieces[0, 3]
    for n in range(1, nz):
        color = [color[c] + trans * pieces[n, c] for c in range(3)]
        trans = trans * pieces[n, 3]
    for c in range(3):
        out_ref[c] = color[c]
    out_ref[3] = trans

    for condition, copy in copies:
        if condition is None:
            copy.wait_send()
        else:
            pl.when(condition)(copy.wait_send)


def on_device(volume, centers, sharpness, extinction, colors):
    nx, nz = lax.axis_size("gx"), lax.axis_size("gz")
    depth, rows, columns = volume.shape
    groups = depth // (columns // HALO)
    row_block = rows // nz
    bound = 3.0 * centers.shape[0] / (depth * nz)
    terms = 1
    while bound ** terms / math.factorial(terms + 1) > 2.0 ** -26:
        terms += 1
    left, main, edge = constants(rows, columns)
    dma = pltpu.SemaphoreType.DMA
    slab = (rows, columns)
    return pl.pallas_call(
        functools.partial(kernel, nx, nz, terms),
        out_shape=jax.ShapeDtypeStruct((4, row_block, columns), F32),
        in_specs=[pl.BlockSpec(memory_space=pltpu.HBM)] * 8,
        out_specs=pl.BlockSpec(memory_space=pltpu.VMEM),
        scratch_shapes=[
            pltpu.SMEM(centers.shape, F32),
            pltpu.SMEM(sharpness.shape, F32),
            pltpu.SMEM(extinction.shape, F32),
            pltpu.SMEM(colors.shape, F32),
            pltpu.VMEM(left.shape, BF16),
            pltpu.VMEM(main.shape, BF16),
            pltpu.VMEM(edge.shape, BF16),
            pltpu.VMEM((depth,) + slab, F32),
            pltpu.VMEM((2, groups) + slab, F32),
            pltpu.VMEM((2, 2, 8, columns), F32),
            pltpu.VMEM((2, groups) + slab, F32),
            pltpu.VMEM((2, 2, 8, columns), F32),
            pltpu.VMEM((2, HALO) + slab, F32),
            pltpu.VMEM(((2 * groups + 2) * rows, 3 * columns), BF16),
            pltpu.VMEM((depth + 2 * HALO,) + slab, F32),
            pltpu.VMEM((nz - 1, 4, row_block, columns), F32),
            pltpu.VMEM((nz, 4, row_block, columns), F32),
            dma((2 * groups,)), dma((7,)),
            dma((2, groups)), dma((2, groups)),
            dma((2, 2)), dma((2, 2)),
            dma((2,)), dma((2,)),
            dma((nz - 1,)), dma((nz,)),
        ],
        compiler_params=pltpu.CompilerParams(
            collective_id=0, has_side_effects=True, vmem_limit_bytes=60 * 1024 * 1024
        ),
    )(volume, centers, sharpness, extinction, colors, jnp.asarray(left), jnp.asarray(main), jnp.asarray(edge))


def solution(mesh):
    return jax.shard_map(
        on_device,
        mesh=mesh,
        in_specs=(P("gz", None, "gx"), P(), P(), P(), P()),
        out_specs=P(None, "gz", "gx"),
        check_vma=False,
    )
```

```python
import functools
import math

import jax
import jax.numpy as jnp
import numpy as np
from jax import lax
from jax.experimental import pallas as pl
from jax.experimental.pallas import tpu as pltpu
from jax.sharding import PartitionSpec as P

F32 = jnp.float32
BF16 = jnp.bfloat16
MESH = pl.DeviceIdType.MESH
HALO = 4


def tap_weights():
    raw = [math.exp(-(j * j) / 8.0) for j in range(-4, 5)]
    whole = sum(raw)
    return [value / whole for value in raw]


def split_const(matrix):
    high = matrix.astype(np.float32).astype(BF16)
    low = (matrix - high.astype(np.float64)).astype(np.float32).astype(BF16)
    return high, low


def band(count, shift, rows):
    weights = tap_weights()
    matrix = np.zeros((rows, count), np.float64)
    for source in range(rows):
        for target in range(count):
            offset = shift(source) - target
            if -4 <= offset <= 4:
                matrix[source, target] = weights[offset + 4]
    return matrix


def constants(rows, columns):
    high, low = split_const(band(rows, lambda i: i, rows).T)
    left = np.concatenate([np.concatenate([high, high], axis=1), np.concatenate([low, low], axis=1)], axis=0)
    high, low = split_const(band(columns, lambda i: i, columns))
    main = np.concatenate([np.concatenate([high, high], axis=0), np.concatenate([low, low], axis=0)], axis=1)
    side = band(columns, lambda i: i - HALO if i < HALO else columns + i - HALO, 2 * HALO)
    half = columns // 2
    edges = []
    for m in range(half // HALO):
        spot = np.zeros((columns, columns), np.float64)
        spot[HALO * m:HALO * (m + 1)] = side[:HALO]
        spot[half + HALO * m:half + HALO * (m + 1)] = side[HALO:]
        high, low = split_const(spot)
        edges.append(np.concatenate([high, high, low], axis=0))
    edge = np.stack([np.concatenate(edges[m:m + 2], axis=1) for m in range(0, len(edges), 2)])
    return left, main, edge


def split(value):
    high = value.astype(BF16)
    low = (value - high.astype(F32)).astype(BF16)
    return high, low


def rows_pass(left, slab):
    high, low = split(slab)
    both = jnp.dot(left, jnp.concatenate([high, low], axis=0), preferred_element_type=F32)
    count = both.shape[0] // 2
    return both[:count] + both[count:]


def columns_pass(rows, matrix):
    high, low = split(rows)
    both = jnp.dot(jnp.concatenate([high, low], axis=1), matrix, preferred_element_type=F32)
    count = both.shape[1] // 2
    return both[:, :count] + both[:, count:]


def kernel(nx, nz, terms, volume, centers_in, sharpness_in, extinction_in, colors_in, left_in, main_in, edge_in,
           out_ref, centers, sharpness, extinction, colors, left_ref, main_ref, edge_ref, vol, packed, corner,
           beside, corner_in, layers, tall_ref, smooth, sent, pieces, load_sem, small_sem,
           beside_send, beside_recv, corner_send, corner_recv, layer_send, layer_recv, image_send, image_recv):
    depth, rows, columns = vol.shape
    per_group = columns // HALO
    groups = depth // per_group
    half = columns // 2
    row_block = rows // nz
    ix = lax.axis_index("gx")
    iz = lax.axis_index("gz")
    sides = ((ix < nx - 1, ix + 1), (ix > 0, ix - 1))
    ends = ((iz > 0, iz - 1), (iz < nz - 1, iz + 1))

    barrier = pltpu.get_barrier_semaphore()

    def greet(x, z):
        pl.semaphore_signal(barrier, inc=1, device_id={"gx": x, "gz": z}, device_id_type=MESH)

    for here, x in sides:
        pl.when(here)(functools.partial(greet, x, iz))
        for there, z in ends:
            pl.when(here & there)(functools.partial(greet, x, z))
    for step in range(1, nz):
        greet(ix, lax.rem(iz + step, nz))

    loads = []
    chunk = per_group // 2
    for g in range(2 * groups):
        span = pl.ds(g * chunk, chunk)
        loads.append(pltpu.make_async_copy(volume.at[span], vol.at[span], load_sem.at[g]))
        loads[-1].start()

    smalls = []
    for i, (source, target) in enumerate((
        (left_in, left_ref), (main_in, main_ref), (edge_in, edge_ref), (centers_in, centers),
        (sharpness_in, sharpness), (extinction_in, extinction), (colors_in, colors),
    )):
        smalls.append(pltpu.make_async_copy(source, target, small_sem.at[i]))
        smalls[-1].start()

    lane = lax.broadcasted_iota(jnp.int32, (rows, columns), 1)
    lane8 = lax.broadcasted_iota(jnp.int32, (8, columns), 1)
    corner_lanes = HALO * HALO

    def remote(source, target, send, recv, x, z):
        return pltpu.make_async_remote_copy(
            src_ref=source, dst_ref=target, send_sem=send, recv_sem=recv,
            device_id={"gx": x, "gz": z}, device_id_type=MESH,
        )

    def arrival(target, send, recv):
        return remote(target, target, send, recv, ix, iz)

    copies = []

    def launch(condition, copy):
        copies.append((condition, copy))
        pl.when(condition)(copy.start)

    for g in range(groups):
        totals = [jnp.zeros((rows, columns), F32)] * 2
        for m in range(per_group):
            if m % chunk == 0:
                loads[(g * per_group + m) // chunk].wait()
            plane = vol[g * per_group + m]
            for side, shift in ((0, HALO * m + HALO), (1, HALO * m)):
                shift = shift % columns
                turned = pltpu.roll(plane, shift, axis=1) if shift else plane
                totals[side] = jnp.where(lane // HALO == m, turned, totals[side])
        for side in range(2):
            packed[side, g] = totals[side]
        if g == 0:
            count = nz - 1
            for here, x in sides:
                span = 1 + ends[0][0].astype(jnp.int32) + ends[1][0].astype(jnp.int32)
                count = count + here.astype(jnp.int32) * span
            pl.semaphore_wait(barrier, count)
        for side, (here, x) in enumerate(sides):
            launch(here, remote(packed.at[side, g], beside.at[side, g], beside_send.at[side, g], beside_recv.at[side, g], x, iz))
        if g == 0:
            for end, (there, z) in enumerate(ends):
                edge_span = pl.ds(0 if end == 0 else depth - HALO, HALO)
                launch(there, remote(volume.at[edge_span], layers.at[1 - end], layer_send.at[end], layer_recv.at[1 - end], ix, z))
        for end, (there, z) in enumerate(ends):
            if g != (0 if end == 0 else groups - 1):
                continue
            first = 0 if end == 0 else columns - corner_lanes
            for side, (here, x) in enumerate(sides):
                small = jnp.zeros((8, columns), F32)
                for t in range(rows // 8):
                    shift = (corner_lanes * t - first) % columns
                    turned = totals[side][8 * t:8 * t + 8]
                    turned = pltpu.roll(turned, shift, axis=1) if shift else turned
                    small = jnp.where(lane8 // corner_lanes == t, turned, small)
                corner[side, end] = small
                launch(here & there, remote(
                    corner.at[side, end], corner_in.at[side, 1 - end],
                    corner_send.at[side, end], corner_recv.at[side, 1 - end], x, z,
                ))

    for small in smalls:
        small.wait()
    left = left_ref[...]

    def plane_pass(source, start, target):
        wide = jnp.concatenate([source[start + i] for i in range(HALO)], axis=1)
        wide = rows_pass(left, wide)
        tall = jnp.concatenate([wide[:, i * columns:(i + 1) * columns] for i in range(HALO)], axis=0)
        tall = columns_pass(tall, main_ref[...])
        for i in range(HALO):
            smooth[target + i] = tall[i * rows:(i + 1) * rows]

    @pl.loop(0, depth // HALO, unroll=8)
    def _(step):
        plane_pass(vol, step * HALO, step * HALO + HALO)

    def arrive(condition, copy, inbox):
        pl.when(condition)(copy.wait_recv)

        @pl.when(jnp.logical_not(condition))
        def _():
            inbox[...] = jnp.zeros(inbox.shape, F32)

    for end, (there, z) in enumerate(ends):
        arrive(there, arrival(layers.at[end], layer_send.at[end], layer_recv.at[end]), layers.at[end])
        plane_pass(layers.at[end], 0, end * (depth + HALO))

    for side in range(2):
        here = sides[1 - side][0]
        for g in range(groups):
            slot = (side, g)
            arrive(here, arrival(beside.at[slot], beside_send.at[slot], beside_recv.at[slot]), beside.at[slot])
        for end, (there, z) in enumerate(ends):
            slot = (side, end)
            arrive(here & there, arrival(corner_in.at[slot], corner_send.at[slot], corner_recv.at[slot]), corner_in.at[slot])

    blocks = []
    for g in range(groups):
        near, far = beside[0, g], beside[1, g]
        blocks.append(jnp.where(lane < half, near, pltpu.roll(far, half, axis=1)))
        blocks.append(jnp.where(lane < half, pltpu.roll(near, half, axis=1), far))
    for end in range(2):
        spread = []
        for t in range(rows // 8):
            shift = (columns - corner_lanes * t) % columns
            near = pltpu.roll(corner_in[0, end], shift, axis=1) if shift else corner_in[0, end]
            shift = (columns + half - corner_lanes * t) % columns
            far = pltpu.roll(corner_in[1, end], shift, axis=1) if shift else corner_in[1, end]
            spread.append(jnp.where(lane8 < half, near, far))
        blocks.append(jnp.concatenate(spread, axis=0))
    wide = rows_pass(left, jnp.concatenate(blocks, axis=1))
    high, low = split(jnp.concatenate([wide[:, i * columns:(i + 1) * columns] for i in range(len(blocks))], axis=0))
    tall_ref[...] = jnp.concatenate([high, low, high], axis=1)
    per_block = half // HALO

    def edges(pair, block, count, places):
        part = jnp.dot(tall_ref[block * rows:(block + count) * rows], edge_ref[pair], preferred_element_type=F32)
        for p, place in enumerate(places):
            for i in range(2):
                smooth[place + i] += part[p * rows:(p + 1) * rows, i * columns:(i + 1) * columns]

    for pair in range(HALO // 2):
        edges(pair, 2 * groups, 2, [2 * pair, depth + HALO + 2 * pair])

    @pl.loop(0, per_block // 2, unroll=8)
    def _(pair):
        edges(pair, 0, 2 * groups, [HALO + p * per_block + 2 * pair for p in range(2 * groups)])

    taps = tap_weights()
    comps = centers.shape[0]
    cells = depth * nz
    middle = [centers[k] for k in range(comps)]
    fall = [sharpness[k] * F32(-math.log2(math.e)) for k in range(comps)]
    absorb = [extinction[k] * F32(1.0 / cells) for k in range(comps)]
    shine = [[colors[c, k] for k in range(comps)] for c in range(3)]
    unroll = 4

    def render(row):
        start = pl.multiple_of(row * row_block, row_block)

        def body(step, carry):
            trans, red, green, blue = carry
            z = step * unroll

            def load(j):
                return smooth[pl.ds(z + j, unroll), pl.ds(start, row_block), :]

            density = taps[4] * load(4)
            for j in range(4):
                density = density + taps[j] * (load(j) + load(8 - j))
            tau = None
            for k in range(comps):
                offset = density - middle[k]
                bump = jnp.exp2(fall[k] * offset * offset)
                if tau is None:
                    tau = absorb[k] * bump
                    emits = [shine[c][k] * bump for c in range(3)]
                else:
                    tau = tau + absorb[k] * bump
                    emits = [emits[c] + shine[c][k] * bump for c in range(3)]
            series = tau * ((-1.0) ** (terms - 1) / math.factorial(terms))
            for n in range(terms - 1, 0, -1):
                series = (series + (-1.0) ** (n - 1) / math.factorial(n)) * tau
            for i in range(unroll):
                weight = trans * series[i]
                trans = trans - weight
                red = red + weight * emits[0][i]
                green = green + weight * emits[1][i]
                blue = blue + weight * emits[2][i]
            return trans, red, green, blue

        none = jnp.zeros((row_block, columns), F32)
        trans, red, green, blue = lax.fori_loop(0, depth // unroll, body, (none + 1.0, none, none, none))
        return red, green, blue, trans

    for step in range(1, nz):
        peer = lax.rem(iz + step, nz)
        for c, plane in enumerate(render(peer)):
            sent[step - 1, c] = plane
        copy = remote(sent.at[step - 1], pieces.at[iz], image_send.at[step - 1], image_recv.at[iz], ix, peer)
        copy.start()
        copies.append((None, copy))
    for c, plane in enumerate(render(iz)):
        pieces[iz, c] = plane

    for step in range(1, nz):
        peer = lax.rem(iz + step, nz)
        remote(pieces.at[peer], pieces.at[peer], image_send.at[step - 1], image_recv.at[peer], ix, peer).wait_recv()

    color = [pieces[0, c] for c in range(3)]
    trans = pieces[0, 3]
    for n in range(1, nz):
        color = [color[c] + trans * pieces[n, c] for c in range(3)]
        trans = trans * pieces[n, 3]
    for c in range(3):
        out_ref[c] = color[c]
    out_ref[3] = trans

    for condition, copy in copies:
        if condition is None:
            copy.wait_send()
        else:
            pl.when(condition)(copy.wait_send)


def on_device(volume, centers, sharpness, extinction, colors):
    nx, nz = lax.axis_size("gx"), lax.axis_size("gz")
    depth, rows, columns = volume.shape
    groups = depth // (columns // HALO)
    row_block = rows // nz
    bound = 3.0 * centers.shape[0] / (depth * nz)
    terms = 1
    while bound ** terms / math.factorial(terms + 1) > 2.0 ** -26:
        terms += 1
    left, main, edge = constants(rows, columns)
    dma = pltpu.SemaphoreType.DMA
    slab = (rows, columns)
    return pl.pallas_call(
        functools.partial(kernel, nx, nz, terms),
        out_shape=jax.ShapeDtypeStruct((4, row_block, columns), F32),
        in_specs=[pl.BlockSpec(memory_space=pltpu.HBM)] * 8,
        out_specs=pl.BlockSpec(memory_space=pltpu.VMEM),
        scratch_shapes=[
            pltpu.SMEM(centers.shape, F32),
            pltpu.SMEM(sharpness.shape, F32),
            pltpu.SMEM(extinction.shape, F32),
            pltpu.SMEM(colors.shape, F32),
            pltpu.VMEM(left.shape, BF16),
            pltpu.VMEM(main.shape, BF16),
            pltpu.VMEM(edge.shape, BF16),
            pltpu.VMEM((depth,) + slab, F32),
            pltpu.VMEM((2, groups) + slab, F32),
            pltpu.VMEM((2, 2, 8, columns), F32),
            pltpu.VMEM((2, groups) + slab, F32),
            pltpu.VMEM((2, 2, 8, columns), F32),
            pltpu.VMEM((2, HALO) + slab, F32),
            pltpu.VMEM(((2 * groups + 2) * rows, 3 * columns), BF16),
            pltpu.VMEM((depth + 2 * HALO,) + slab, F32),
            pltpu.VMEM((nz - 1, 4, row_block, columns), F32),
            pltpu.VMEM((nz, 4, row_block, columns), F32),
            dma((2 * groups,)), dma((7,)),
            dma((2, groups)), dma((2, groups)),
            dma((2, 2)), dma((2, 2)),
            dma((2,)), dma((2,)),
            dma((nz - 1,)), dma((nz,)),
        ],
        compiler_params=pltpu.CompilerParams(
            collective_id=0, has_side_effects=True, vmem_limit_bytes=60 * 1024 * 1024
        ),
    )(volume, centers, sharpness, extinction, colors, jnp.asarray(left), jnp.asarray(main), jnp.asarray(edge))


def solution(mesh):
    return jax.shard_map(
        on_device,
        mesh=mesh,
        in_specs=(P("gz", None, "gx"), P(), P(), P(), P()),
        out_specs=P(None, "gz", "gx"),
        check_vma=False,
    )
```
